128 devices in a mesh: chan: 16 (over z, x_lo, core), seg: 8 (over y, x_hi).
Axes of the slice: x: 4 (x_hi: 2, x_lo: 2; x = x_hi * 2 + x_lo), y: 4, z: 4, core: 2. Of those that a mesh axis runs over, the one named last changes fastest.
Arguments:
- record: bfloat16 [144000, 6144], P('seg', 'chan'), may hold values from -24 to 24
- offsets: int32 [24], P('seg'), may hold values from 0 to 64
- bins: int32 [128], replicated, may hold values from 1 to 5999
- band_limit: int32 [6144], P('chan'), may hold values from 50 to 200
Outputs:
- stacked: bfloat16 [200, 2, 128, 6144], P(None, None, 'seg', 'chan')
The draws below stay inside these ranges and needn't reach their ends.
All inputs are finite; a program needn't handle non-finite values.
Results may differ from the reference program's by a relative error of at most 0.0069.
Values may be sent and summed in bfloat16 or wider, within the bound.
A program may use at most 192 MiB of HBM per device.

```python
import math
import jax
import jax.numpy as jnp
from jax import lax

SEG_LEN = 12000
HOP = 6000
SLACK = 64
BINS = 128
LAGS = 200
CHANNELS = 6144
SEGS = 24
TIME = 144000


def draw_record(key, part):
    key_noise = jax.random.fold_in(key, 11)
    key_common = jax.random.fold_in(key, 12)
    key_amp = jax.random.fold_in(key, 13)
    position = jnp.arange(CHANNELS, dtype=jnp.float32)[None, :] / CHANNELS
    noise = jax.random.normal(key_noise, (TIME, CHANNELS), jnp.float32)
    spread = jnp.exp(jax.random.uniform(key_amp, (1, CHANNELS), jnp.float32, -1.1, 1.1))
    common = 1.5 * jax.random.normal(key_common, (TIME, 1), jnp.float32)
    values = common + noise * spread * (1.0 + 2.0 * position)
    return jnp.clip(values, -24.0, 24.0).astype(jnp.bfloat16)


def draw_offsets(key, part):
    values = jax.random.randint(jax.random.fold_in(key, 21), (SEGS,), 0, SLACK + 1, jnp.int32)
    return values.at[0].set(0).at[1].set(SLACK)


def draw_band_limit(key, part):
    values = jax.random.randint(jax.random.fold_in(key, 31), (CHANNELS,), LAGS // 4, LAGS + 1, jnp.int32)
    return values.at[0].set(LAGS)


def set_ends(array, own_key, least, high):
    shape = array.shape
    spot = [jax.random.randint(jax.random.fold_in(own_key, axis), (), 0, shape[axis]) for axis in range(len(shape))]
    array = array.at[tuple(spot)].set(least)
    longest = shape.index(max(shape))
    spot[longest] = (spot[longest] + 1) % shape[longest]
    return array.at[tuple(spot)].set(high)


def setup_inputs(seed: int = 0) -> dict:
    splits = jax.random.split(jax.random.key(seed), 5)
    record = draw_record(jax.random.fold_in(splits[4], 71), 0)
    offsets = draw_offsets(jax.random.fold_in(splits[4], 71), 0)
    bins = set_ends(jax.random.randint(splits[2], (BINS,), 1, HOP), jax.random.fold_in(splits[2], 1), 1, HOP - 1).astype(jnp.int32)
    band_limit = draw_band_limit(jax.random.fold_in(splits[4], 71), 0)
    return dict(record=record, offsets=offsets, bins=bins, band_limit=band_limit)


def table_of(bins):
    times = jnp.arange(SEG_LEN, dtype=jnp.int32)[:, None]
    phase = times * bins.astype(jnp.int32)[None, :] % SEG_LEN
    angle = phase.astype(jnp.float32) * (2.0 * math.pi / SEG_LEN)
    return jnp.concatenate([jnp.cos(angle), -jnp.sin(angle)], axis=1).astype(jnp.bfloat16)

def reference(record, offsets, bins, band_limit):
    table = table_of(bins)

    def one_segment(index):
        start = index * HOP + offsets[index]
        rows = start + jnp.arange(SEG_LEN, dtype=jnp.int32)
        window = jnp.take(record, rows, axis=0, mode='fill', fill_value=0)
        wide = window.astype(jnp.float32)
        common = lax.optimization_barrier(jnp.sum(wide, axis=1, keepdims=True)) / CHANNELS
        cleaned = (wide - common).astype(jnp.bfloat16)
        spectrum = jnp.dot(table.T, cleaned, preferred_element_type=jnp.float32)
        power = lax.optimization_barrier(jnp.mean(spectrum * spectrum, axis=0, keepdims=True))
        white = (spectrum * lax.rsqrt(power + 1e-06)).astype(jnp.bfloat16)
        return white.reshape(2, BINS, CHANNELS)
    spectra = lax.map(one_segment, jnp.arange(SEGS, dtype=jnp.int32))
    extended = jnp.concatenate([spectra, jnp.zeros((SEGS, 2, BINS, LAGS), jnp.bfloat16)], axis=3)

    def one_lag(lag):
        other = lax.dynamic_slice_in_dim(extended, lag, CHANNELS, 3).astype(jnp.float32)
        own = spectra.astype(jnp.float32)
        real_part = lax.optimization_barrier(jnp.sum(own[:, 0] * other[:, 0] + own[:, 1] * other[:, 1], axis=0))
        imag_part = lax.optimization_barrier(jnp.sum(own[:, 1] * other[:, 0] - own[:, 0] * other[:, 1], axis=0))
        keep = (band_limit >= lag).astype(jnp.float32) / SEGS
        return (jnp.stack([real_part, imag_part]) * keep[None, None, :]).astype(jnp.bfloat16)
    return lax.map(one_lag, jnp.arange(LAGS, dtype=jnp.int32))
```

```python
import math

import jax
import jax.numpy as jnp
from jax import lax
from jax.experimental import pallas as pl
from jax.experimental.pallas import tpu as pltpu
from jax.sharding import PartitionSpec as P

SEG_LEN = 12000
HOP = 6000
LAGS = 200
RIM = 128
CHUNK = 1024
CHUNKS = -(-HOP // CHUNK)
BLOCKS = CHUNK // 128
LAST = HOP - CHUNK
VMEM_LIMIT = 60 * 1024 * 1024
F32 = jnp.float32
BF16 = jnp.bfloat16


def dot(a, b, dims):
    return lax.dot_general(a, b, (dims, ((), ())), preferred_element_type=F32)


def dft_kernel(offs_ref, bins_ref, rec_ref, nxt_ref, out_ref, x_ref, fine, coarse, w_ref, acc, sems):
    def piece(i, block):
        lo = CHUNK * i
        size = min(CHUNK, HOP - lo)
        rows = pl.ds(HOP * block + lo, size)
        return pltpu.make_async_copy(rec_ref.at[rows], x_ref.at[rows], sems.at[i, block])

    for i in range(CHUNKS):
        for block in range(3):
            piece(i, block).start()

    bcol = jnp.transpose(jnp.broadcast_to(bins_ref[...].astype(F32), (128, 128))).astype(jnp.int32)
    lane = lax.broadcasted_iota(jnp.int32, (128, 128), 1)

    def phasor(times):
        phase = (bcol * times) % SEG_LEN
        angle = phase.astype(F32) * (2.0 * math.pi / SEG_LEN)
        return jnp.cos(angle), -jnp.sin(angle)

    base_c, base_s = phasor(lane)
    column = lane - BLOCKS
    owner = column // CHUNKS
    step = column - owner * CHUNKS
    start = jnp.minimum(step * CHUNK, LAST)
    shift = jnp.where(
        owner == 0,
        offs_ref[0],
        jnp.where(owner == 1, offs_ref[1], jnp.where(owner == 2, offs_ref[2], offs_ref[3])),
    )
    times = jnp.where(lane < BLOCKS, lane * 128, start - shift + SEG_LEN)
    times = jnp.where(lane < BLOCKS + 4 * CHUNKS, times, 0) % SEG_LEN
    mult_c, mult_s = phasor(times)

    def spread(values, index):
        return jnp.broadcast_to(values[:, index : index + 1], (128, 128))

    def rotate(ac, as_, bc, bs):
        return ac * bc - as_ * bs, as_ * bc + ac * bs

    for m in range(BLOCKS):
        c, s = rotate(spread(mult_c, m), spread(mult_s, m), base_c, base_s)
        fine[0, m] = c
        fine[1, m] = s
    for q in range(4 * CHUNKS):
        coarse[q, 0] = spread(mult_c, BLOCKS + q)
        coarse[q, 1] = spread(mult_s, BLOCKS + q)

    acc[...] = jnp.zeros_like(acc)

    def chunk(i, carry):
        first = jnp.minimum(i * CHUNK, LAST)
        skip = i * CHUNK - first
        for block in range(3):
            for j in range(CHUNKS):
                @pl.when(i == j)
                def _():
                    piece(j, block).wait()
        for o in range(4):
            ec = coarse[o * CHUNKS + i, 0]
            es = coarse[o * CHUNKS + i, 1]
            for m in range(BLOCKS):
                c, s = rotate(ec, es, fine[0, m], fine[1, m])
                if m < 2:
                    live = lane + 128 * m >= skip
                    c = jnp.where(live, c, 0.0)
                    s = jnp.where(live, s, 0.0)
                w_ref[pl.ds(256 * o, 128), pl.ds(128 * m, 128)] = c.astype(BF16)
                w_ref[pl.ds(256 * o + 128, 128), pl.ds(128 * m, 128)] = s.astype(BF16)
        for block in range(3):
            rows = x_ref[pl.ds(pl.multiple_of(HOP * block + first, 16), CHUNK), :]
            acc[block] += dot(w_ref[pl.ds(256 * block, 512), :], rows, ((1,), (0,)))
        return carry

    lax.fori_loop(0, CHUNKS, chunk, 0)

    def head(o):
        c, s = rotate(coarse[o * CHUNKS, 0], coarse[o * CHUNKS, 1], fine[0, 0], fine[1, 0])
        live = lane < offs_ref[o]
        zero = jnp.zeros_like(c)
        return jnp.concatenate([jnp.where(live, c, zero), jnp.where(live, s, zero)], axis=0)

    def first_rows(block):
        return x_ref[pl.ds(HOP * block, RIM), :]

    def swap(o, new, old):
        w = head(o).astype(BF16)
        both = jnp.concatenate([w, -w], axis=1)
        return dot(both, jnp.concatenate([new, old], axis=0), ((1,), (0,)))

    odd = jnp.concatenate([bcol, bcol], axis=0) % 2
    sign = (1 - 2 * odd).astype(F32)
    sign = jnp.concatenate([sign, sign, sign], axis=1)
    out_ref[0] = sign * acc[0, :256] + dot(head(0).astype(BF16), first_rows(1), ((1,), (0,)))
    out_ref[1] = acc[0, 256:] + sign * acc[1, :256] + swap(1, first_rows(2), first_rows(0))
    out_ref[2] = acc[1, 256:] + sign * acc[2, :256] + swap(2, nxt_ref[...], first_rows(1))
    out_ref[3] = acc[2, 256:] - dot(head(3).astype(BF16), first_rows(2), ((1,), (0,)))


def partial_spectra(offs, bins, record, nxt):
    width = record.shape[1]
    vmem = pl.BlockSpec(memory_space=pltpu.VMEM)
    return pl.pallas_call(
        dft_kernel,
        out_shape=jax.ShapeDtypeStruct((4, 256, width), F32),
        in_specs=[pl.BlockSpec(memory_space=pltpu.SMEM), vmem, pl.BlockSpec(memory_space=pl.ANY), vmem],
        out_specs=vmem,
        scratch_shapes=[
            pltpu.VMEM(record.shape, BF16),
            pltpu.VMEM((2, BLOCKS, 128, 128), F32),
            pltpu.VMEM((4 * CHUNKS, 2, 128, 128), F32),
            pltpu.VMEM((1024, CHUNK), BF16),
            pltpu.VMEM((3, 512, width), F32),
            pltpu.SemaphoreType.DMA((CHUNKS, 3)),
        ],
        compiler_params=pltpu.CompilerParams(vmem_limit_bytes=VMEM_LIMIT),
        name="dft",
    )(offs, bins, record, nxt)


def band_kernel(scale, ext_ref, limit_ref, out_ref, own, rev, wide):
    tile = pl.program_id(0)
    rows = own.shape[1]
    segs = rows // 32

    @pl.when(tile == 0)
    def _():
        size = rev.shape[0] * 128
        at = lax.broadcasted_iota(jnp.int32, (size, size), 0)
        to = lax.broadcasted_iota(jnp.int32, (size, size), 1)
        flip = (at + to == size - 1).astype(BF16)
        turned = dot(ext_ref[...], flip, ((1,), (0,)))
        for t in range(rev.shape[0]):
            rev[t] = turned[:, 128 * t : 128 * t + 128]
        for t in range(own.shape[0]):
            own[t] = ext_ref[:, 128 * t : 128 * t + 128].astype(F32)

    lag = lax.broadcasted_iota(jnp.int32, (208, 256), 0)
    spot = lax.broadcasted_iota(jnp.int32, (208, 256), 1)
    pick = (lag + spot == 255).astype(BF16)
    back = own.shape[0] - 1 - tile

    def one_bin(f, carry):
        real = own[tile, pl.ds(f, segs, stride=32), :]
        imag = own[tile, pl.ds(16 + f, segs, stride=32), :]
        lhs = jnp.concatenate(
            [jnp.concatenate([real, imag], axis=0), jnp.concatenate([imag, -real], axis=0)], axis=1
        ).astype(BF16)
        other = []
        for t in range(3):
            other.append(
                jnp.concatenate(
                    [rev[back + t, pl.ds(f, segs, stride=32), :], rev[back + t, pl.ds(16 + f, segs, stride=32), :]],
                    axis=0,
                )
            )
        rhs = jnp.concatenate(other, axis=1).astype(BF16)
        product = dot(lhs, rhs, ((0,), (0,)))
        lined = []
        for p in range(2):
            rolled = pltpu.roll(product[128 * p : 128 * p + 128], 0, 1, stride=1, stride_axis=0)
            lined.append((rolled[:, 128:] * scale).astype(BF16))
        by_lag = dot(pick, jnp.concatenate(lined, axis=0), ((1,), (1,)))
        wide[pl.ds(f, LAGS, stride=32), :] = by_lag[:LAGS, :128]
        wide[pl.ds(16 + f, LAGS, stride=32), :] = by_lag[:LAGS, 128:]
        return carry

    lax.fori_loop(0, 16, one_bin, 0)
    limit = jnp.broadcast_to(limit_ref[...], (32, 128))

    def store(j, carry):
        for n in range(8):
            k = j * 8 + n
            values = wide[pl.ds(pl.multiple_of(k * 32, 32), 32), :]
            values = jnp.where(limit >= k, values, 0.0).astype(BF16)
            out_ref[k, 0] = values[:16]
            out_ref[k, 1] = values[16:]
        return carry

    lax.fori_loop(0, LAGS // 8, store, 0)


def band(ext, limit, segs, width):
    rows, reach = ext.shape
    return pl.pallas_call(
        lambda *refs: band_kernel(1.0 / segs, *refs),
        grid=(width // 128,),
        out_shape=jax.ShapeDtypeStruct((LAGS, 2, 16, width), BF16),
        in_specs=[
            pl.BlockSpec((rows, reach), lambda i: (0, 0)),
            pl.BlockSpec((1, 128), lambda i: (0, i)),
        ],
        out_specs=pl.BlockSpec((LAGS, 2, 16, 128), lambda i: (0, 0, 0, i)),
        scratch_shapes=[
            pltpu.VMEM((width // 128, rows, 128), F32),
            pltpu.VMEM((reach // 128, rows, 128), F32),
            pltpu.VMEM((LAGS * 32, 128), F32),
        ],
        compiler_params=pltpu.CompilerParams(vmem_limit_bytes=VMEM_LIMIT),
        name="band",
    )(ext, limit)


def along(shard, axis, by):
    count = lax.axis_size(axis)
    pairs = [(i, i + by) for i in range(count) if 0 <= i + by < count]
    return lax.ppermute(shard, axis, pairs)


def shards(record, offsets, bins, band_limit):
    width = record.shape[1]
    segs = offsets.shape[0] * lax.axis_size("seg")
    channels = width * lax.axis_size("chan")
    nxt = along(record[:RIM], "seg", -1)
    before = along(offsets, "seg", 1)
    offs = jnp.concatenate([before[2:], offsets])
    parts = partial_spectra(offs, bins[None, :], record, nxt)
    rest = along(parts[0], "seg", -1)
    spectra = jnp.stack([parts[1], parts[2], parts[3] + rest])
    mean = lax.psum(jnp.sum(spectra, axis=2), "chan") / channels
    spectra = spectra - mean[:, :, None]
    power = jnp.mean(spectra * spectra, axis=1, keepdims=True)
    white = (spectra * lax.rsqrt(power + 1e-06)).astype(BF16).reshape(3, 2, 128, width)
    regrouped = lax.all_to_all(white, "seg", split_axis=2, concat_axis=0, tiled=True)
    neighbour = along(regrouped[..., :256], "chan", -1)
    ext = jnp.concatenate([regrouped, neighbour], axis=3)
    return band(ext.reshape(segs * 32, width + 256), band_limit[None, :], segs, width)


def solution(mesh):
    return jax.shard_map(
        shards,
        mesh=mesh,
        in_specs=(P("seg", "chan"), P("seg"), P(), P("chan")),
        out_specs=P(None, None, "seg", "chan"),
        check_vma=False,
    )
```

```python
import functools
import math

import jax
import jax.numpy as jnp
from jax import lax
from jax.experimental import pallas as pl
from jax.experimental.pallas import tpu as pltpu
from jax.sharding import PartitionSpec as P

SEG_LEN = 12000
HOP = 6000
LAGS = 200
PITCH = 33
UNROLL = 4
RIM = 64
CHUNK = 1024
CHUNKS = -(-HOP // CHUNK)
BLOCKS = CHUNK // 128
LAST = HOP - CHUNK
VMEM_LIMIT = 60 * 1024 * 1024
F32 = jnp.float32
BF16 = jnp.bfloat16
MESH = pl.DeviceIdType.MESH


def dot(a, b, dims):
    return lax.dot_general(a, b, (dims, ((), ())), preferred_element_type=F32)


def spectra_kernel(
    chans, segs, offs_ref, bins_ref, rec_ref, out_ref,
    x_ref, fine, coarse, w_ref, acc, accs, spec, head, lump, first_sum, first_sums, own_sum, own_sums,
    rim, rest, white, got,
    local_sem, rim_send, rim_recv, lump_send, lump_recv, first_send, first_recv, sum_send, sum_recv,
    part_send, part_recv, near_send, near_recv,
):
    me_c = lax.axis_index("chan")
    me_s = lax.axis_index("seg")
    before = (me_s + segs - 1) % segs
    after = (me_s + 1) % segs
    left = (me_c + chans - 1) % chans
    width = x_ref.shape[1]

    rim[:, RIM:, :] = jnp.zeros((2, 128 - RIM, width), BF16)

    barrier = pltpu.get_barrier_semaphore()

    def greet(c, g):
        pl.semaphore_signal(barrier, inc=1, device_id={"chan": c, "seg": g}, device_id_type=MESH)

    def greet_chan(i, carry):
        c = (me_c + i) % chans
        greet(c, me_s)
        greet(c, before)
        greet(c, after)
        return carry

    def greet_seg(i, carry):
        greet(me_c, (me_s + i) % segs)
        return carry

    lax.fori_loop(1, chans, greet_chan, 0)
    lax.fori_loop(1, segs, greet_seg, 0)

    def piece(block, i, size):
        rows = pl.ds(pl.multiple_of(HOP * block + CHUNK * i, 16), size)
        return pltpu.make_async_copy(rec_ref.at[rows], x_ref.at[rows], local_sem.at[block, i])

    for block in range(3):
        for i in range(CHUNKS):
            piece(block, i, CHUNK if i < CHUNKS - 1 else HOP - CHUNK * (CHUNKS - 1)).start()

    bcol = jnp.transpose(jnp.broadcast_to(bins_ref[...].astype(F32), (128, 128))).astype(jnp.int32)
    lane = lax.broadcasted_iota(jnp.int32, (128, 128), 1)

    def phasor(times):
        phase = (bcol * times) % SEG_LEN
        angle = phase.astype(F32) * (2.0 * math.pi / SEG_LEN)
        return jnp.cos(angle), -jnp.sin(angle)

    base_c, base_s = phasor(lane)
    times = jnp.where(lane < BLOCKS, lane * 128, jnp.minimum((lane - BLOCKS) * CHUNK, LAST))
    for q in range(3):
        times = jnp.where(lane == BLOCKS + CHUNKS + q, SEG_LEN - offs_ref[q], times)
    mult_c, mult_s = phasor(times % SEG_LEN)

    def spread(values, index):
        return jnp.broadcast_to(values[:, index : index + 1], (128, 128))

    def rotate(ac, as_, bc, bs):
        return ac * bc - as_ * bs, as_ * bc + ac * bs

    for m in range(BLOCKS):
        c, s = rotate(spread(mult_c, m), spread(mult_s, m), base_c, base_s)
        fine[0, m] = c
        fine[1, m] = s
    for q in range(CHUNKS + 3):
        coarse[q, 0] = spread(mult_c, BLOCKS + q)
        coarse[q, 1] = spread(mult_s, BLOCKS + q)
    odd = bcol % 2
    sign = (1 - 2 * odd).astype(F32)

    pl.semaphore_wait(barrier, 3 * (chans - 1) + segs - 1)

    def send_rim(k):
        return pltpu.make_async_remote_copy(
            src_ref=rec_ref.at[pl.ds(HOP * k, RIM)],
            dst_ref=rim.at[k, pl.ds(0, RIM)],
            send_sem=rim_send.at[k],
            recv_sem=rim_recv.at[k],
            device_id={"chan": me_c, "seg": before},
            device_id_type=MESH,
        )

    for k in range(2):
        send_rim(k).start()

    acc[...] = jnp.zeros_like(acc)
    accs[...] = jnp.zeros_like(accs)

    def build(i, skip):
        ec = coarse[i, 0]
        es = coarse[i, 1]
        for m in range(BLOCKS):
            c, s = rotate(ec, es, fine[0, m], fine[1, m])
            if skip > 128 * m:
                live = lane + 128 * m >= skip
                c = jnp.where(live, c, 0.0)
                s = jnp.where(live, s, 0.0)
            w_ref[i, :128, pl.ds(128 * m, 128)] = c.astype(BF16)
            w_ref[i, 128:, pl.ds(128 * m, 128)] = s.astype(BF16)

    def rows(block, first):
        return pl.ds(pl.multiple_of(HOP * block + first, 16), CHUNK)

    def block_zero(i, first):
        acc[...] += dot(w_ref[i], x_ref[rows(0, first), :], ((1,), (0,)))

    def early(i, carry):
        piece(0, i, CHUNK).wait()
        build(i, 0)
        block_zero(i, i * CHUNK)
        return carry

    final = CHUNKS - 1
    lax.fori_loop(0, final, early, 0)
    piece(0, final, HOP - CHUNK * final).wait()
    build(final, final * CHUNK - LAST)
    block_zero(final, LAST)

    def sum_row(values):
        folded = values[:, :128]
        for t in range(1, width // 128):
            folded = folded + values[:, 128 * t : 128 * t + 128]
        return jnp.sum(jnp.transpose(folded), axis=0, keepdims=True)

    def column(row):
        return jnp.transpose(jnp.broadcast_to(row, (128, 128)))

    def wide(tile):
        return jnp.concatenate([tile] * (width // 128), axis=1)

    for p in range(2):
        values = acc[pl.ds(128 * p, 128), :]
        row = sum_row(values)
        first_sum[pl.ds(p, 1), :] = row
        lump[pl.ds(128 * p, 128), :] = (values - wide(column(row) * (1.0 / width))).astype(BF16)
    first_sum[2:, :] = jnp.zeros((6, 128), F32)

    send_lump = pltpu.make_async_remote_copy(
        src_ref=lump,
        dst_ref=rest,
        send_sem=lump_send,
        recv_sem=lump_recv,
        device_id={"chan": me_c, "seg": before},
        device_id_type=MESH,
    )

    def send_first(i):
        return pltpu.make_async_remote_copy(
            src_ref=first_sum,
            dst_ref=first_sums.at[i],
            send_sem=first_send.at[i],
            recv_sem=first_recv.at[i],
            device_id={"chan": (me_c + i) % chans, "seg": before},
            device_id_type=MESH,
        )

    def send_sum(i):
        return pltpu.make_async_remote_copy(
            src_ref=own_sum,
            dst_ref=own_sums.at[i],
            send_sem=sum_send.at[i],
            recv_sem=sum_recv.at[i],
            device_id={"chan": (me_c + i) % chans, "seg": me_s},
            device_id_type=MESH,
        )

    def started(make):
        def body(i, carry):
            make(i).start()
            return carry
        return body

    def received(make):
        def body(i, carry):
            make(i).wait_recv()
            return carry
        return body

    def sent(make):
        def body(i, carry):
            make(i).wait_send()
            return carry
        return body

    lax.fori_loop(0, chans, started(send_first), 0)
    send_lump.start()

    def later(i, first):
        table = w_ref[i]
        for block in (1, 2):
            accs[block - 1] += dot(table, x_ref[rows(block, first), :256], ((1,), (0,)))
        tails = jnp.concatenate([x_ref[rows(1, first), 256:], x_ref[rows(2, first), 256:]], axis=1)
        accs[2] += dot(table, tails, ((1,), (0,)))

    def late(i, carry):
        for block in (1, 2):
            piece(block, i, CHUNK).wait()
        later(i, i * CHUNK)
        return carry

    lax.fori_loop(0, final, late, 0)
    for block in (1, 2):
        piece(block, final, HOP - CHUNK * final).wait()
    later(final, LAST)

    edge = w_ref[0, :, pl.ds(0, 128)].astype(F32)
    lane2 = lax.broadcasted_iota(jnp.int32, (256, 128), 1)
    alive = jnp.where(me_s == segs - 1, 0.0, 1.0).astype(F32)

    def swap(q, new, old):
        table = jnp.where(lane2 < offs_ref[q], edge, 0.0)
        both = jnp.concatenate([table, -table], axis=1).astype(BF16)
        head[...] = dot(both, jnp.concatenate([new, old], axis=0), ((1,), (0,)))

    def block_sum(p, parts):
        at = pl.ds(128 * p, 128)
        total = head[at, :]
        for factor, block in parts:
            if block == 0:
                values = acc[at, :]
            else:
                values = jnp.concatenate(
                    [accs[block - 1, at, :], accs[2, at, pl.ds(128 * (block - 1), 128)]], axis=1
                )
            total = total + (values if factor is None else values * factor)
        return total

    def finish(q, parts):
        c = block_sum(0, parts)
        s = block_sum(1, parts)
        c, s = rotate(c, s, wide(coarse[CHUNKS + q, 0]), wide(coarse[CHUNKS + q, 1]))
        spec[q, :128] = c
        spec[q, 128:] = s
        own_sum[pl.ds(2 * q, 1), :] = sum_row(c)
        own_sum[pl.ds(2 * q + 1, 1), :] = sum_row(s)

    def first_rows(block):
        return x_ref[pl.ds(HOP * block, 128), :]

    def rim_rows(k):
        return (rim[k].astype(F32) * alive).astype(BF16)

    own_sum[6:, :] = jnp.zeros((2, 128), F32)
    signs = wide(sign)
    swap(0, first_rows(2), first_rows(0))
    finish(0, [(None, 0), (signs, 1)])
    send_rim(0).wait_recv()
    swap(1, rim_rows(0), first_rows(1))
    finish(1, [(None, 1), (signs, 2)])
    send_rim(1).wait_recv()
    swap(2, rim_rows(1), first_rows(2))
    finish(2, [(None, 2)])
    lax.fori_loop(1, chans, started(send_sum), 0)

    lax.fori_loop(0, chans, received(send_first), 0)
    first_total = first_sums[0]
    for i in range(1, chans):
        first_total = first_total + first_sums[i]
    mine = first_sums[0] * (1.0 / width)
    send_lump.wait_recv()
    turn_c = coarse[CHUNKS + 2, 0]
    turn_s = coarse[CHUNKS + 2, 1]
    flip = sign * alive
    rest_c = (rest[:128, :].astype(F32) + wide(column(mine[0:1]))) * wide(flip)
    rest_s = (rest[128:, :].astype(F32) + wide(column(mine[1:2]))) * wide(flip)
    rest_c, rest_s = rotate(rest_c, rest_s, wide(turn_c), wide(turn_s))
    spec[2, :128] += rest_c
    spec[2, 128:] += rest_s

    lax.fori_loop(1, chans, received(send_sum), 0)
    total = own_sum[...]
    for i in range(1, chans):
        total = total + own_sums[i]
    scale = 1.0 / (width * chans)

    def send_part(q, i):
        g = (me_s + i) % segs
        return pltpu.make_async_remote_copy(
            src_ref=white.at[q, :, pl.ds(pl.multiple_of(16 * g, 16), 16), :],
            dst_ref=got.at[me_s, q, :, :, pl.ds(0, width)],
            send_sem=part_send.at[q, i],
            recv_sem=part_recv.at[q, i],
            device_id={"chan": me_c, "seg": g},
            device_id_type=MESH,
        )

    def take_part(q, i):
        g = (me_s + segs - i) % segs
        return pltpu.make_async_remote_copy(
            src_ref=white.at[q, :, pl.ds(0, 16), :],
            dst_ref=got.at[g, q, :, :, pl.ds(0, width)],
            send_sem=part_send.at[q, i],
            recv_sem=part_recv.at[q, i],
            device_id={"chan": me_c, "seg": g},
            device_id_type=MESH,
        )

    def send_near(q, i):
        g = (me_s + segs - i) % segs
        return pltpu.make_async_remote_copy(
            src_ref=got.at[g, q, :, :, pl.ds(0, 256)],
            dst_ref=got.at[g, q, :, :, pl.ds(width, 256)],
            send_sem=near_send.at[q, i],
            recv_sem=near_recv.at[q, i],
            device_id={"chan": left, "seg": me_s},
            device_id_type=MESH,
        )

    for q in range(3):
        mean_c = column(total[2 * q : 2 * q + 1] * scale)
        mean_s = column(total[2 * q + 1 : 2 * q + 2] * scale)
        if q == 2:
            more_c, more_s = rotate(
                column(first_total[0:1] * scale) * flip, column(first_total[1:2] * scale) * flip, turn_c, turn_s
            )
            mean_c = mean_c + more_c
            mean_s = mean_s + more_s
        c = spec[q, :128] - wide(mean_c)
        s = spec[q, 128:] - wide(mean_s)
        power = jnp.sum(c * c + s * s, axis=0, keepdims=True) * (1.0 / 256)
        gain = lax.rsqrt(power + 1e-06)
        white[q, 0] = (c * gain).astype(BF16)
        white[q, 1] = (s * gain).astype(BF16)
        lax.fori_loop(1, segs, started(lambda i: send_part(q, i)), 0)
        mine_at = pl.ds(pl.multiple_of(16 * me_s, 16), 16)
        for p in range(2):
            got[me_s, q, p, :, pl.ds(0, width)] = white[q, p, mine_at, :]
        send_near(q, 0).start()

    for q in range(3):
        def relay(i, carry):
            take_part(q, i).wait_recv()
            send_near(q, i).start()
            return carry
        lax.fori_loop(1, segs, relay, 0)
    for q in range(3):
        lax.fori_loop(0, segs, received(lambda i: send_near(q, i)), 0)
    shown = jnp.where(me_c == chans - 1, 0.0, 1.0).astype(F32)

    def put(g, carry):
        for q in range(3):
            for p in range(2):
                out_ref[g, q, p, :, pl.ds(0, width)] = got[g, q, p, :, pl.ds(0, width)]
                tail = got[g, q, p, :, pl.ds(width, 256)].astype(F32) * shown
                out_ref[g, q, p, :, pl.ds(width, 256)] = tail.astype(BF16)
        return carry

    lax.fori_loop(0, segs, put, 0)

    for k in range(2):
        send_rim(k).wait_send()
    send_lump.wait_send()
    lax.fori_loop(0, chans, sent(send_first), 0)
    lax.fori_loop(1, chans, sent(send_sum), 0)
    for q in range(3):
        lax.fori_loop(1, segs, sent(lambda i: send_part(q, i)), 0)
        lax.fori_loop(0, segs, sent(lambda i: send_near(q, i)), 0)


def spectra(offsets, bins, record, chans, segs):
    width = record.shape[1]
    vmem = pl.BlockSpec(memory_space=pltpu.VMEM)
    sems = pltpu.SemaphoreType.DMA
    return pl.pallas_call(
        functools.partial(spectra_kernel, chans, segs),
        out_shape=jax.ShapeDtypeStruct((segs, 3, 2, 16, width + 256), BF16),
        in_specs=[pl.BlockSpec(memory_space=pltpu.SMEM), vmem, pl.BlockSpec(memory_space=pl.ANY)],
        out_specs=vmem,
        scratch_shapes=[
            pltpu.VMEM(record.shape, BF16),
            pltpu.VMEM((2, BLOCKS, 128, 128), F32),
            pltpu.VMEM((CHUNKS + 3, 2, 128, 128), F32),
            pltpu.VMEM((CHUNKS, 256, CHUNK), BF16),
            pltpu.VMEM((256, width), F32),
            pltpu.VMEM((3, 256, 256), F32),
            pltpu.VMEM((3, 256, width), F32),
            pltpu.VMEM((256, width), F32),
            pltpu.VMEM((256, width), BF16),
            pltpu.VMEM((8, 128), F32),
            pltpu.VMEM((chans, 8, 128), F32),
            pltpu.VMEM((8, 128), F32),
            pltpu.VMEM((chans, 8, 128), F32),
            pltpu.VMEM((2, 128, width), BF16),
            pltpu.VMEM((256, width), BF16),
            pltpu.VMEM((3, 2, 128, width), BF16),
            pltpu.VMEM((segs, 3, 2, 16, width + 256), BF16),
            sems((3, CHUNKS)),
            sems((2,)),
            sems((2,)),
            sems(()),
            sems(()),
            sems((chans,)),
            sems((chans,)),
            sems((chans,)),
            sems((chans,)),
            sems((3, segs)),
            sems((3, segs)),
            sems((3, segs)),
            sems((3, segs)),
        ],
        compiler_params=pltpu.CompilerParams(
            vmem_limit_bytes=VMEM_LIMIT, collective_id=0, has_side_effects=True
        ),
        name="spectra",
    )(offsets, bins, record)


def band_kernel(scale, ext_ref, limit_ref, out_ref, own, rev, wide):
    tile = pl.program_id(0)
    segs = ext_ref.shape[0] // 32

    @pl.when(tile == 0)
    def _():
        size = rev.shape[0] * 128
        at = lax.broadcasted_iota(jnp.int32, (size, size), 0)
        to = lax.broadcasted_iota(jnp.int32, (size, size), 1)
        flip = (at + to == size - 1).astype(BF16)
        turned = dot(ext_ref[...], flip, ((1,), (0,)))
        for t in range(rev.shape[0]):
            for n in range(segs):
                rev[t, pl.ds(PITCH * n, 32)] = turned[32 * n : 32 * n + 32, 128 * t : 128 * t + 128]
        for t in range(own.shape[0]):
            for n in range(segs):
                own[t, pl.ds(PITCH * n, 32)] = ext_ref[32 * n : 32 * n + 32, 128 * t : 128 * t + 128].astype(F32)

    lag = lax.broadcasted_iota(jnp.int32, (208, 256), 0)
    spot = lax.broadcasted_iota(jnp.int32, (208, 256), 1)
    pick = (lag + spot == 255).astype(BF16)
    back = own.shape[0] - 1 - tile

    def one_bin(f, carry):
        real = own[tile, pl.ds(f, segs, stride=PITCH), :]
        imag = own[tile, pl.ds(16 + f, segs, stride=PITCH), :]
        lhs = jnp.concatenate(
            [jnp.concatenate([real, imag], axis=0), jnp.concatenate([imag, -real], axis=0)], axis=1
        ).astype(BF16)
        other = []
        for t in range(3):
            other.append(
                jnp.concatenate(
                    [rev[back + t, pl.ds(f, segs, stride=PITCH), :], rev[back + t, pl.ds(16 + f, segs, stride=PITCH), :]],
                    axis=0,
                )
            )
        rhs = jnp.concatenate(other, axis=1).astype(BF16)
        product = dot(lhs, rhs, ((0,), (0,)))
        lined = []
        for p in range(2):
            rolled = pltpu.roll(product[128 * p : 128 * p + 128], 0, 1, stride=1, stride_axis=0)
            lined.append((rolled[:, 128:] * scale).astype(BF16))
        by_lag = dot(pick, jnp.concatenate(lined, axis=0), ((1,), (1,)))
        wide[pl.ds(f, LAGS, stride=PITCH), :] = by_lag[:LAGS, :128]
        wide[pl.ds(16 + f, LAGS, stride=PITCH), :] = by_lag[:LAGS, 128:]
        return carry

    lax.fori_loop(0, 16, one_bin, 0, unroll=UNROLL)
    limit = jnp.broadcast_to(limit_ref[...], (32, 128))

    def store(j, carry):
        for n in range(8):
            k = j * 8 + n
            values = wide[pl.ds(k * PITCH, 32), :]
            values = jnp.where(limit >= k, values, 0.0).astype(BF16)
            out_ref[k, 0] = values[:16]
            out_ref[k, 1] = values[16:]
        return carry

    lax.fori_loop(0, LAGS // 8, store, 0)


def band(ext, limit, segs, width):
    rows, reach = ext.shape
    return pl.pallas_call(
        lambda *refs: band_kernel(1.0 / segs, *refs),
        grid=(width // 128,),
        out_shape=jax.ShapeDtypeStruct((LAGS, 2, 16, width), BF16),
        in_specs=[
            pl.BlockSpec((rows, reach), lambda i: (0, 0)),
            pl.BlockSpec((1, 128), lambda i: (0, i)),
        ],
        out_specs=pl.BlockSpec((LAGS, 2, 16, 128), lambda i: (0, 0, 0, i)),
        scratch_shapes=[
            pltpu.VMEM((width // 128, segs * PITCH, 128), F32),
            pltpu.VMEM((reach // 128, segs * PITCH, 128), F32),
            pltpu.VMEM((LAGS * PITCH, 128), F32),
        ],
        compiler_params=pltpu.CompilerParams(vmem_limit_bytes=VMEM_LIMIT),
        name="band",
    )(ext, limit)


def shards(record, offsets, bins, band_limit):
    width = record.shape[1]
    segs = lax.axis_size("seg")
    parts = spectra(offsets, bins[None, :], record, lax.axis_size("chan"), segs)
    ext = parts.reshape(segs * 96, width + 256)
    return band(ext, band_limit[None, :], segs * 3, width)


def solution(mesh):
    return jax.shard_map(
        shards,
        mesh=mesh,
        in_specs=(P("seg", "chan"), P("seg"), P(), P("chan")),
        out_specs=P(None, None, "seg", "chan"),
        check_vma=False,
    )
```

```python
import functools
import math

import jax
import jax.numpy as jnp
from jax import lax
from jax.experimental import pallas as pl
from jax.experimental.pallas import tpu as pltpu
from jax.sharding import PartitionSpec as P

SEG_LEN = 12000
HOP = 6000
LAGS = 200
PITCH = 33
UNROLL = 4
RIM = 64
CHUNK = 1024
CHUNKS = -(-HOP // CHUNK)
BLOCKS = CHUNK // 128
LAST = HOP - CHUNK
VMEM_LIMIT = 60 * 1024 * 1024
F32 = jnp.float32
BF16 = jnp.bfloat16
MESH = pl.DeviceIdType.MESH


def dot(a, b, dims):
    return lax.dot_general(a, b, (dims, ((), ())), preferred_element_type=F32)


def spectra_kernel(
    chans, segs, offs_ref, bins_ref, rec_ref, out_ref,
    x_ref, fine, coarse, w_ref, acc, accs, spec, head, lump, first_sum, first_sums, own_sum, own_sums,
    rest_sum, group_sum, rim, rest, white, got,
    local_sem, rim_send, rim_recv, row_send, row_recv, lump_send, lump_recv, first_send, first_recv, sum_send, sum_recv,
    part_send, part_recv, near_send, near_recv,
):
    me_c = lax.axis_index("chan")
    me_s = lax.axis_index("seg")
    before = (me_s + segs - 1) % segs
    left = (me_c + chans - 1) % chans
    width = x_ref.shape[1]

    rim[:, RIM:, :] = jnp.zeros((2, 128 - RIM, width), BF16)

    barrier = pltpu.get_barrier_semaphore()

    def greet(c, g):
        pl.semaphore_signal(barrier, inc=1, device_id={"chan": c, "seg": g}, device_id_type=MESH)

    def greet_chan(i, carry):
        greet((me_c + i) % chans, me_s)
        return carry

    def greet_seg(i, carry):
        greet(me_c, (me_s + i) % segs)
        return carry

    lax.fori_loop(1, chans, greet_chan, 0)
    lax.fori_loop(1, segs, greet_seg, 0)

    def piece(block, i, size):
        rows = pl.ds(pl.multiple_of(HOP * block + CHUNK * i, 16), size)
        return pltpu.make_async_copy(rec_ref.at[rows], x_ref.at[rows], local_sem.at[block, i])

    for block in range(3):
        for i in range(CHUNKS):
            piece(block, i, CHUNK if i < CHUNKS - 1 else HOP - CHUNK * (CHUNKS - 1)).start()

    bcol = jnp.transpose(jnp.broadcast_to(bins_ref[...].astype(F32), (128, 128))).astype(jnp.int32)
    lane = lax.broadcasted_iota(jnp.int32, (128, 128), 1)

    def phasor(times):
        phase = (bcol * times) % SEG_LEN
        angle = phase.astype(F32) * (2.0 * math.pi / SEG_LEN)
        return jnp.cos(angle), -jnp.sin(angle)

    base_c, base_s = phasor(lane)
    times = jnp.where(lane < BLOCKS, lane * 128, jnp.minimum((lane - BLOCKS) * CHUNK, LAST))
    for q in range(3):
        times = jnp.where(lane == BLOCKS + CHUNKS + q, SEG_LEN - offs_ref[q], times)
    mult_c, mult_s = phasor(times % SEG_LEN)

    def spread(values, index):
        return jnp.broadcast_to(values[:, index : index + 1], (128, 128))

    def rotate(ac, as_, bc, bs):
        return ac * bc - as_ * bs, as_ * bc + ac * bs

    for m in range(BLOCKS):
        c, s = rotate(spread(mult_c, m), spread(mult_s, m), base_c, base_s)
        fine[0, m] = c
        fine[1, m] = s
    for q in range(CHUNKS + 3):
        coarse[q, 0] = spread(mult_c, BLOCKS + q)
        coarse[q, 1] = spread(mult_s, BLOCKS + q)
    odd = bcol % 2
    sign = (1 - 2 * odd).astype(F32)

    def send_rim(k):
        return pltpu.make_async_remote_copy(
            src_ref=rec_ref.at[pl.ds(HOP * k, RIM)],
            dst_ref=rim.at[k, pl.ds(0, RIM)],
            send_sem=rim_send.at[k],
            recv_sem=rim_recv.at[k],
            device_id={"chan": me_c, "seg": before},
            device_id_type=MESH,
        )

    acc[...] = jnp.zeros_like(acc)
    accs[...] = jnp.zeros_like(accs)

    def build(i, skip):
        ec = coarse[i, 0]
        es = coarse[i, 1]
        for m in range(BLOCKS):
            c, s = rotate(ec, es, fine[0, m], fine[1, m])
            if skip > 128 * m:
                live = lane + 128 * m >= skip
                c = jnp.where(live, c, 0.0)
                s = jnp.where(live, s, 0.0)
            w_ref[i, :128, pl.ds(128 * m, 128)] = c.astype(BF16)
            w_ref[i, 128:, pl.ds(128 * m, 128)] = s.astype(BF16)

    def rows(block, first):
        return pl.ds(pl.multiple_of(HOP * block + first, 16), CHUNK)

    def block_zero(i, first):
        acc[...] += dot(w_ref[i], x_ref[rows(0, first), :], ((1,), (0,)))

    def early(i, carry):
        piece(0, i, CHUNK).wait()
        build(i, 0)
        block_zero(i, i * CHUNK)
        return carry

    final = CHUNKS - 1
    lax.fori_loop(0, final, early, 0)
    piece(0, final, HOP - CHUNK * final).wait()
    build(final, final * CHUNK - LAST)
    block_zero(final, LAST)

    def sum_row(values):
        folded = values[:, :128]
        for t in range(1, width // 128):
            folded = folded + values[:, 128 * t : 128 * t + 128]
        return jnp.sum(jnp.transpose(folded), axis=0, keepdims=True)

    def column(row):
        return jnp.transpose(jnp.broadcast_to(row, (128, 128)))

    def wide(tile):
        return jnp.concatenate([tile] * (width // 128), axis=1)

    for p in range(2):
        values = acc[pl.ds(128 * p, 128), :]
        row = sum_row(values)
        first_sum[pl.ds(p, 1), :] = row
        lump[pl.ds(128 * p, 128), :] = (values - wide(column(row) * (1.0 / width))).astype(BF16)
    first_sum[2:, :] = jnp.zeros((6, 128), F32)

    send_lump = pltpu.make_async_remote_copy(
        src_ref=lump,
        dst_ref=rest,
        send_sem=lump_send,
        recv_sem=lump_recv,
        device_id={"chan": me_c, "seg": before},
        device_id_type=MESH,
    )

    def send_first(i):
        return pltpu.make_async_remote_copy(
            src_ref=first_sum,
            dst_ref=first_sums.at[i],
            send_sem=first_send.at[i],
            recv_sem=first_recv.at[i],
            device_id={"chan": (me_c + i) % chans, "seg": me_s},
            device_id_type=MESH,
        )

    def send_sum(i):
        return pltpu.make_async_remote_copy(
            src_ref=own_sum,
            dst_ref=own_sums.at[i],
            send_sem=sum_send.at[i],
            recv_sem=sum_recv.at[i],
            device_id={"chan": (me_c + i) % chans, "seg": me_s},
            device_id_type=MESH,
        )

    def started(make):
        def body(i, carry):
            make(i).start()
            return carry
        return body

    def received(make):
        def body(i, carry):
            make(i).wait_recv()
            return carry
        return body

    def sent(make):
        def body(i, carry):
            make(i).wait_send()
            return carry
        return body

    def send_row(k, source):
        return pltpu.make_async_remote_copy(
            src_ref=source,
            dst_ref=rest_sum.at[k],
            send_sem=row_send.at[k],
            recv_sem=row_recv.at[k],
            device_id={"chan": me_c, "seg": before},
            device_id_type=MESH,
        )

    pl.semaphore_wait(barrier, chans + segs - 2)
    lax.fori_loop(1, chans, started(send_first), 0)
    send_row(0, first_sum).start()
    send_lump.start()
    for k in range(2):
        send_rim(k).start()

    def later(i, first):
        table = w_ref[i]
        for block in (1, 2):
            accs[block - 1] += dot(table, x_ref[rows(block, first), :256], ((1,), (0,)))
        tails = jnp.concatenate([x_ref[rows(1, first), 256:], x_ref[rows(2, first), 256:]], axis=1)
        accs[2] += dot(table, tails, ((1,), (0,)))

    def late(i, carry):
        for block in (1, 2):
            piece(block, i, CHUNK).wait()
        later(i, i * CHUNK)
        return carry

    lax.fori_loop(0, final, late, 0)
    for block in (1, 2):
        piece(block, final, HOP - CHUNK * final).wait()
    later(final, LAST)

    lax.fori_loop(1, chans, received(send_first), 0)
    first_total = first_sum[...]
    for i in range(1, chans):
        first_total = first_total + first_sums[i]
    group_sum[...] = first_total
    send_row(1, group_sum).start()

    edge = w_ref[0, :, pl.ds(0, 128)].astype(F32)
    lane2 = lax.broadcasted_iota(jnp.int32, (256, 128), 1)
    alive = jnp.where(me_s == segs - 1, 0.0, 1.0).astype(F32)

    def swap(q, new, old):
        table = jnp.where(lane2 < offs_ref[q], edge, 0.0)
        both = jnp.concatenate([table, -table], axis=1).astype(BF16)
        head[...] = dot(both, jnp.concatenate([new, old], axis=0), ((1,), (0,)))

    def block_sum(p, parts):
        at = pl.ds(128 * p, 128)
        total = head[at, :]
        for factor, block in parts:
            if block == 0:
                values = acc[at, :]
            else:
                values = jnp.concatenate(
                    [accs[block - 1, at, :], accs[2, at, pl.ds(128 * (block - 1), 128)]], axis=1
                )
            total = total + (values if factor is None else values * factor)
        return total

    def finish(q, parts):
        c = block_sum(0, parts)
        s = block_sum(1, parts)
        c, s = rotate(c, s, wide(coarse[CHUNKS + q, 0]), wide(coarse[CHUNKS + q, 1]))
        spec[q, :128] = c
        spec[q, 128:] = s
        own_sum[pl.ds(2 * q, 1), :] = sum_row(c)
        own_sum[pl.ds(2 * q + 1, 1), :] = sum_row(s)

    def first_rows(block):
        return x_ref[pl.ds(HOP * block, 128), :]

    def rim_rows(k):
        return (rim[k].astype(F32) * alive).astype(BF16)

    own_sum[6:, :] = jnp.zeros((2, 128), F32)
    signs = wide(sign)
    swap(0, first_rows(2), first_rows(0))
    finish(0, [(None, 0), (signs, 1)])
    send_rim(0).wait_recv()
    swap(1, rim_rows(0), first_rows(1))
    finish(1, [(None, 1), (signs, 2)])
    send_rim(1).wait_recv()
    swap(2, rim_rows(1), first_rows(2))
    finish(2, [(None, 2)])
    lax.fori_loop(1, chans, started(send_sum), 0)

    scale = 1.0 / (width * chans)
    send_row(0, first_sum).wait_recv()
    mine = rest_sum[0] * (1.0 / width)
    send_lump.wait_recv()
    turn_c = coarse[CHUNKS + 2, 0]
    turn_s = coarse[CHUNKS + 2, 1]
    flip = sign * alive
    rest_c = (rest[:128, :].astype(F32) + wide(column(mine[0:1]))) * wide(flip)
    rest_s = (rest[128:, :].astype(F32) + wide(column(mine[1:2]))) * wide(flip)
    rest_c, rest_s = rotate(rest_c, rest_s, wide(turn_c), wide(turn_s))
    spec[2, :128] += rest_c
    spec[2, 128:] += rest_s

    lax.fori_loop(1, chans, received(send_sum), 0)
    send_row(1, group_sum).wait_recv()
    behind = rest_sum[1] * scale
    total = own_sum[...]
    for i in range(1, chans):
        total = total + own_sums[i]

    def send_part(q, i):
        g = (me_s + i) % segs
        return pltpu.make_async_remote_copy(
            src_ref=white.at[q, :, pl.ds(pl.multiple_of(16 * g, 16), 16), :],
            dst_ref=got.at[me_s, q, :, :, pl.ds(0, width)],
            send_sem=part_send.at[q, i],
            recv_sem=part_recv.at[q, i],
            device_id={"chan": me_c, "seg": g},
            device_id_type=MESH,
        )

    def take_part(q, i):
        g = (me_s + segs - i) % segs
        return pltpu.make_async_remote_copy(
            src_ref=white.at[q, :, pl.ds(0, 16), :],
            dst_ref=got.at[g, q, :, :, pl.ds(0, width)],
            send_sem=part_send.at[q, i],
            recv_sem=part_recv.at[q, i],
            device_id={"chan": me_c, "seg": g},
            device_id_type=MESH,
        )

    def send_near(q, i):
        g = (me_s + segs - i) % segs
        return pltpu.make_async_remote_copy(
            src_ref=got.at[g, q, :, :, pl.ds(0, 256)],
            dst_ref=got.at[g, q, :, :, pl.ds(width, 256)],
            send_sem=near_send.at[q, i],
            recv_sem=near_recv.at[q, i],
            device_id={"chan": left, "seg": me_s},
            device_id_type=MESH,
        )

    for q in range(3):
        mean_c = column(total[2 * q : 2 * q + 1] * scale)
        mean_s = column(total[2 * q + 1 : 2 * q + 2] * scale)
        if q == 2:
            more_c, more_s = rotate(
                column(behind[0:1]) * flip, column(behind[1:2]) * flip, turn_c, turn_s
            )
            mean_c = mean_c + more_c
            mean_s = mean_s + more_s
        c = spec[q, :128] - wide(mean_c)
        s = spec[q, 128:] - wide(mean_s)
        power = jnp.sum(c * c + s * s, axis=0, keepdims=True) * (1.0 / 256)
        gain = lax.rsqrt(power + 1e-06)
        white[q, 0] = (c * gain).astype(BF16)
        white[q, 1] = (s * gain).astype(BF16)
        lax.fori_loop(1, segs, started(lambda i: send_part(q, i)), 0)
        mine_at = pl.ds(pl.multiple_of(16 * me_s, 16), 16)
        for p in range(2):
            got[me_s, q, p, :, pl.ds(0, width)] = white[q, p, mine_at, :]
        send_near(q, 0).start()

    for q in range(3):
        def relay(i, carry):
            take_part(q, i).wait_recv()
            send_near(q, i).start()
            return carry
        lax.fori_loop(1, segs, relay, 0)
    for q in range(3):
        lax.fori_loop(0, segs, received(lambda i: send_near(q, i)), 0)
    shown = jnp.where(me_c == chans - 1, 0.0, 1.0).astype(F32)

    def put(g, carry):
        for q in range(3):
            for p in range(2):
                out_ref[g, q, p, :, pl.ds(0, width)] = got[g, q, p, :, pl.ds(0, width)]
                tail = got[g, q, p, :, pl.ds(width, 256)].astype(F32) * shown
                out_ref[g, q, p, :, pl.ds(width, 256)] = tail.astype(BF16)
        return carry

    lax.fori_loop(0, segs, put, 0)

    for k in range(2):
        send_rim(k).wait_send()
    send_lump.wait_send()
    lax.fori_loop(1, chans, sent(send_first), 0)
    send_row(0, first_sum).wait_send()
    send_row(1, group_sum).wait_send()
    lax.fori_loop(1, chans, sent(send_sum), 0)
    for q in range(3):
        lax.fori_loop(1, segs, sent(lambda i: send_part(q, i)), 0)
        lax.fori_loop(0, segs, sent(lambda i: send_near(q, i)), 0)


def spectra(offsets, bins, record, chans, segs):
    width = record.shape[1]
    vmem = pl.BlockSpec(memory_space=pltpu.VMEM)
    sems = pltpu.SemaphoreType.DMA
    return pl.pallas_call(
        functools.partial(spectra_kernel, chans, segs),
        out_shape=jax.ShapeDtypeStruct((segs, 3, 2, 16, width + 256), BF16),
        in_specs=[pl.BlockSpec(memory_space=pltpu.SMEM), vmem, pl.BlockSpec(memory_space=pl.ANY)],
        out_specs=vmem,
        scratch_shapes=[
            pltpu.VMEM(record.shape, BF16),
            pltpu.VMEM((2, BLOCKS, 128, 128), F32),
            pltpu.VMEM((CHUNKS + 3, 2, 128, 128), F32),
            pltpu.VMEM((CHUNKS, 256, CHUNK), BF16),
            pltpu.VMEM((256, width), F32),
            pltpu.VMEM((3, 256, 256), F32),
            pltpu.VMEM((3, 256, width), F32),
            pltpu.VMEM((256, width), F32),
            pltpu.VMEM((256, width), BF16),
            pltpu.VMEM((8, 128), F32),
            pltpu.VMEM((chans, 8, 128), F32),
            pltpu.VMEM((8, 128), F32),
            pltpu.VMEM((chans, 8, 128), F32),
            pltpu.VMEM((2, 8, 128), F32),
            pltpu.VMEM((8, 128), F32),
            pltpu.VMEM((2, 128, width), BF16),
            pltpu.VMEM((256, width), BF16),
            pltpu.VMEM((3, 2, 128, width), BF16),
            pltpu.VMEM((segs, 3, 2, 16, width + 256), BF16),
            sems((3, CHUNKS)),
            sems((2,)),
            sems((2,)),
            sems((2,)),
            sems((2,)),
            sems(()),
            sems(()),
            sems((chans,)),
            sems((chans,)),
            sems((chans,)),
            sems((chans,)),
            sems((3, segs)),
            sems((3, segs)),
            sems((3, segs)),
            sems((3, segs)),
        ],
        compiler_params=pltpu.CompilerParams(
            vmem_limit_bytes=VMEM_LIMIT, collective_id=0, has_side_effects=True
        ),
        name="spectra",
    )(offsets, bins, record)


def band_kernel(scale, ext_ref, limit_ref, out_ref, own, rev, wide):
    tile = pl.program_id(0)
    segs = ext_ref.shape[0] // 32

    @pl.when(tile == 0)
    def _():
        size = rev.shape[0] * 128
        at = lax.broadcasted_iota(jnp.int32, (size, size), 0)
        to = lax.broadcasted_iota(jnp.int32, (size, size), 1)
        flip = (at + to == size - 1).astype(BF16)
        turned = dot(ext_ref[...], flip, ((1,), (0,)))
        for t in range(rev.shape[0]):
            for n in range(segs):
                rev[t, pl.ds(PITCH * n, 32)] = turned[32 * n : 32 * n + 32, 128 * t : 128 * t + 128]
        for t in range(own.shape[0]):
            for n in range(segs):
                own[t, pl.ds(PITCH * n, 32)] = ext_ref[32 * n : 32 * n + 32, 128 * t : 128 * t + 128].astype(F32)

    lag = lax.broadcasted_iota(jnp.int32, (208, 256), 0)
    spot = lax.broadcasted_iota(jnp.int32, (208, 256), 1)
    pick = (lag + spot == 255).astype(BF16)
    back = own.shape[0] - 1 - tile

    def one_bin(f, carry):
        real = own[tile, pl.ds(f, segs, stride=PITCH), :]
        imag = own[tile, pl.ds(16 + f, segs, stride=PITCH), :]
        lhs = jnp.concatenate(
            [jnp.concatenate([real, imag], axis=0), jnp.concatenate([imag, -real], axis=0)], axis=1
        ).astype(BF16)
        other = []
        for t in range(3):
            other.append(
                jnp.concatenate(
                    [rev[back + t, pl.ds(f, segs, stride=PITCH), :], rev[back + t, pl.ds(16 + f, segs, stride=PITCH), :]],
                    axis=0,
                )
            )
        rhs = jnp.concatenate(other, axis=1).astype(BF16)
        product = dot(lhs, rhs, ((0,), (0,)))
        lined = []
        for p in range(2):
            rolled = pltpu.roll(product[128 * p : 128 * p + 128], 0, 1, stride=1, stride_axis=0)
            lined.append((rolled[:, 128:] * scale).astype(BF16))
        by_lag = dot(pick, jnp.concatenate(lined, axis=0), ((1,), (1,)))
        wide[pl.ds(f, LAGS, stride=PITCH), :] = by_lag[:LAGS, :128]
        wide[pl.ds(16 + f, LAGS, stride=PITCH), :] = by_lag[:LAGS, 128:]
        return carry

    lax.fori_loop(0, 16, one_bin, 0, unroll=UNROLL)
    limit = jnp.broadcast_to(limit_ref[pl.ds(pl.multiple_of(tile * 128, 128), 128)].reshape(1, 128), (32, 128))

    def store(j, carry):
        for n in range(8):
            k = j * 8 + n
            values = wide[pl.ds(k * PITCH, 32), :]
            values = jnp.where(limit >= k, values, 0.0).astype(BF16)
            out_ref[k, 0] = values[:16]
            out_ref[k, 1] = values[16:]
        return carry

    lax.fori_loop(0, LAGS // 8, store, 0)


def band(ext, limit, segs, width):
    rows, reach = ext.shape
    return pl.pallas_call(
        lambda *refs: band_kernel(1.0 / segs, *refs),
        grid=(width // 128,),
        out_shape=jax.ShapeDtypeStruct((LAGS, 2, 16, width), BF16),
        in_specs=[
            pl.BlockSpec((rows, reach), lambda i: (0, 0)),
            pl.BlockSpec((width,), lambda i: (0,)),
        ],
        out_specs=pl.BlockSpec((LAGS, 2, 16, 128), lambda i: (0, 0, 0, i)),
        scratch_shapes=[
            pltpu.VMEM((width // 128, segs * PITCH, 128), F32),
            pltpu.VMEM((reach // 128, segs * PITCH, 128), F32),
            pltpu.VMEM((LAGS * PITCH, 128), F32),
        ],
        compiler_params=pltpu.CompilerParams(vmem_limit_bytes=VMEM_LIMIT),
        name="band",
    )(ext, limit)


def shards(record, offsets, bins, band_limit):
    width = record.shape[1]
    segs = lax.axis_size("seg")
    parts = spectra(offsets, bins[None, :], record, lax.axis_size("chan"), segs)
    ext = parts.reshape(segs * 96, width + 256)
    return band(ext, band_limit, segs * 3, width)


def solution(mesh):
    return jax.shard_map(
        shards,
        mesh=mesh,
        in_specs=(P("seg", "chan"), P("seg"), P(), P("chan")),
        out_specs=P(None, None, "seg", "chan"),
        check_vma=False,
    )
```
